32 devices in a mesh: expert: 2 (over y), dp: 4 (over z), section: 4 (over x, core).
Axes of the slice: x: 2, y: 2, z: 4, core: 2. Of those that a mesh axis runs over, the one named last changes fastest.
Arguments:
- tokens: bfloat16 [4096, 1280], P(('expert', 'dp', 'section')), may hold values from -6 to 6
- routes: int32 [4096, 1], P(('expert', 'dp', 'section')), may hold values from 0 to 7
- w_router: bfloat16 [1280, 8], replicated, may hold values from -0.15625 to 0.15625
- w_in: bfloat16 [8, 1280, 5120], P(('expert', 'section'), None, 'dp'), may hold values from -0.15625 to 0.15625
- w_out: bfloat16 [8, 5120, 1280], P(('expert', 'section'), 'dp'), may hold values from -0.078125 to 0.078125
- cotangent: bfloat16 [4096, 1280], P(('expert', 'dp', 'section')), may hold values from -6 to 6
Outputs:
- moe_out: bfloat16 [4096, 1280], P(('expert', 'dp', 'section'))
- router_grad: float32 [1280, 8], replicated
- grad_w_in: bfloat16 [8, 1280, 5120], P(('expert', 'section'), None, 'dp')
- grad_w_out: bfloat16 [8, 5120, 1280], P(('expert', 'section'), 'dp')
The draws below stay inside these ranges and needn't reach their ends.
Inputs may be any that keep to these rules, and one draw needn't show every extreme that they name: `routes`: each token names one expert; every expert is named by some token.
All inputs are finite; a program needn't handle non-finite values.
Results may differ from the reference program's by a relative error of at most 0.019.
Values may be sent and summed in bfloat16 or wider, within the bound.
A program may use at most 64 MiB of HBM per device.

```python
import math
import jax
import jax.numpy as jnp
from jax import lax

D = 1280
FF = 5120
TOK_DEV = 128
EXPERTS = 8
CAP = 12
TOKENS = 4096
N_EXPERT = 2
N_DP = 4
N_SECTION = 4


def levels(own_key, extent, shards, smallest, top_value):
    loudness = 1.0
    for axis_at, shards_of in shards:
        steps = jax.random.uniform(jax.random.fold_in(jax.random.fold_in(own_key, 6), axis_at), (shards_of,), jnp.float32, smallest / len(shards), top_value / len(shards))
        loudness = loudness * jnp.repeat(jnp.exp(steps), extent[axis_at] // shards_of).reshape((-1,) + (1,) * (len(extent) - 1 - axis_at))
    return loudness


def picks_of(own_key, rows, amount, top, lift):
    sequence = jax.random.permutation(jax.random.fold_in(own_key, 1), amount)
    boost = sequence
    for power in range(3):
        boost = boost * boost // amount
    boost = boost * lift // amount
    lots = jax.random.randint(jax.random.fold_in(own_key, 2), (rows, amount), 0, 4096) + boost
    sure = jax.random.permutation(jax.random.fold_in(own_key, 3), rows)[jnp.arange(amount) % rows]
    lots = jnp.where(jnp.arange(rows)[:, None] == sure[None, :], 1 << 14, lots)
    merit = lots * amount + jnp.arange(amount)
    return lax.top_k(merit.astype(jnp.int32), top)[1].astype(jnp.int32)


def bell_draw(stream_key, shape, scale, most, split=(), kind=jnp.bfloat16):
    level = levels(stream_key, shape, split, -0.22, 0.18) if split else 1.0
    entries = jax.random.normal(stream_key, shape, jnp.float32) * scale * level
    return jnp.minimum(jnp.maximum(entries, -most), most).astype(kind)


def setup_inputs(seed: int = 0) -> dict:
    key_of = jax.random.split(jax.random.key(seed), 7)
    tokens = bell_draw(key_of[0], (TOKENS, D), 1.0, 6.0, ((0, 32),))
    routes = picks_of(key_of[1], TOKENS, EXPERTS, 1, 2048)
    w_router = bell_draw(key_of[2], (D, EXPERTS), D ** -0.5, 0.15625)
    w_in = bell_draw(key_of[3], (EXPERTS, D, FF), D ** -0.5, 0.15625, ((0, 8), (2, 4)))
    w_out = bell_draw(key_of[4], (EXPERTS, FF, D), FF ** -0.5, 0.078125, ((0, 8), (1, 4)))
    cotangent = bell_draw(key_of[5], (TOKENS, D), 1.0, 6.0, ((0, 32),))
    return dict(tokens=tokens, routes=routes, w_router=w_router, w_in=w_in, w_out=w_out, cotangent=cotangent)


def gelu_exact(value):
    return 0.5 * value * (1.0 + lax.erf(value * (1.0 / math.sqrt(2.0))))

def gelu_slope(value):
    return 0.5 * (1.0 + lax.erf(value * (1.0 / math.sqrt(2.0)))) + value * jnp.exp(-0.5 * value * value) * (1.0 / math.sqrt(2.0 * math.pi))

def reference(tokens, routes, w_router, w_in, w_out, cotangent):
    sources = N_EXPERT * N_DP * N_SECTION
    slots_all = EXPERTS * CAP
    scale = math.sqrt(EXPERTS / TOKENS)
    route = routes[:, 0].reshape(sources, TOK_DEV)
    onehot = (route[:, :, None] == jnp.arange(EXPERTS, dtype=jnp.int32)[None, None, :]).astype(jnp.int32)
    ahead = jnp.cumsum(onehot, axis=1) - onehot
    rank = lax.optimization_barrier(jnp.sum(ahead * onehot, axis=2))
    keep = rank < CAP
    place = jnp.where(keep, route * CAP + rank, slots_all).astype(jnp.int32)
    table = jnp.full((sources, slots_all + 1), TOK_DEV, jnp.int32)
    table = table.at[jnp.arange(sources, dtype=jnp.int32)[:, None], place].set(jnp.broadcast_to(jnp.arange(TOK_DEV, dtype=jnp.int32)[None, :], (sources, TOK_DEV)))
    table = table[:, :slots_all]
    logits = jnp.dot(tokens, w_router, preferred_element_type=jnp.float32)
    chosen = jnp.take_along_axis(logits, routes, axis=1)[:, 0]
    gate = jax.nn.sigmoid(chosen)
    gated_cot = (gate[:, None] * cotangent.astype(jnp.float32)).astype(jnp.bfloat16)

    def to_slots(rows):
        padded = jnp.concatenate([rows.reshape(sources, TOK_DEV, D), jnp.zeros((sources, 1, D), rows.dtype)], axis=1)
        picked = jnp.take_along_axis(padded, table[:, :, None], axis=1)
        return picked.reshape(sources, EXPERTS, CAP, D).transpose(1, 0, 2, 3).reshape(EXPERTS, sources * CAP, D)
    expert_in = to_slots(tokens)
    expert_cot = to_slots(gated_cot)
    rows_count = sources * CAP
    block = FF // N_DP

    def one_expert(pack):
        rows, cot_rows, weight_in, weight_out = pack
        hidden_pre = jnp.dot(rows, weight_in, preferred_element_type=jnp.float32)
        act = gelu_exact(hidden_pre).astype(jnp.bfloat16)
        act_blocks = act.reshape(rows_count, N_DP, block).transpose(1, 0, 2).astype(jnp.float32)
        out_blocks = weight_out.reshape(N_DP, block, D).astype(jnp.float32)
        partial_value = jnp.einsum('brf,bfd->brd', act_blocks, out_blocks).astype(jnp.bfloat16)
        out_rows = lax.optimization_barrier(jnp.sum(partial_value.astype(jnp.float32), axis=0)).astype(jnp.bfloat16)
        act_grad = jnp.dot(cot_rows, weight_out.T, preferred_element_type=jnp.float32)
        hidden_grad = (act_grad * gelu_slope(hidden_pre)).astype(jnp.bfloat16)
        grad_in = (jnp.dot(rows.T, hidden_grad, preferred_element_type=jnp.float32) * scale).astype(jnp.bfloat16)
        grad_out = (jnp.dot(act.T, cot_rows, preferred_element_type=jnp.float32) * scale).astype(jnp.bfloat16)
        return (out_rows, grad_in, grad_out)
    expert_out, grad_w_in, grad_w_out = lax.map(one_expert, (expert_in, expert_cot, w_in, w_out))
    back = expert_out.reshape(EXPERTS, sources, CAP, D).transpose(1, 0, 2, 3).reshape(sources, slots_all, D)
    back = jnp.concatenate([back, jnp.zeros((sources, 1, D), back.dtype)], axis=1)
    picked = jnp.take_along_axis(back, place[:, :, None], axis=1).astype(jnp.float32).reshape(TOKENS, D)
    moe_out = (gate[:, None] * picked).astype(jnp.bfloat16)
    gate_grad = lax.optimization_barrier(jnp.sum(cotangent.astype(jnp.float32) * picked, axis=1))
    logit_grad = gate_grad * gate * (1.0 - gate)
    flat_hot = onehot.reshape(TOKENS, EXPERTS).astype(jnp.float32)
    router_grad = jnp.dot(tokens.astype(jnp.float32).T, flat_hot * logit_grad[:, None], precision=lax.Precision.HIGHEST) * scale
    return (moe_out, router_grad, grad_w_in, grad_w_out)
```

```python
import functools
import math

import jax
import jax.numpy as jnp
from jax import lax
from jax.experimental import pallas as pl
from jax.experimental.pallas import tpu as pltpu
from jax.sharding import PartitionSpec as P

MESH = pl.DeviceIdType.MESH
F32 = jnp.float32
BF16 = jnp.bfloat16


def round_up(value, unit):
    return -(-value // unit) * unit


def exchange_kernel(
    dims,
    tok_ref, route_ref, wr_ref, cot_ref, win_hbm, wout_hbm,
    moe_ref, router_ref, rows_out, cots_out, act_out, hg_out,
    win, wout, slots, arrived, rows, act, slope, hg, part, rx, back_send, back, vec, vec_z, vec_p,
    a_send, a_recv, z_right, z_left, z_recv, c_send, c_recv, b_send, b_recv,
    v_send, v_recv, p_send, p_recv, w_sem, o_sem,
):
    n_y, n_z, n_s, cap, capp, blk, n_c, scale = dims
    chk = blk // n_c
    n_p = n_y * n_s
    y, z, s = lax.axis_index("expert"), lax.axis_index("dp"), lax.axis_index("section")
    me = y * n_s + s
    tok_count, width = tok_ref.shape
    padded = n_p * capp

    load_in = pltpu.make_async_copy(win_hbm, win, w_sem.at[0])
    load_out = pltpu.make_async_copy(wout_hbm, wout, w_sem.at[1])
    load_in.start()
    load_out.start()

    def plane_id(q):
        return (q // n_s, z, q % n_s)

    def peer(k):
        return lax.rem(me + k, n_p)

    def source(k):
        return lax.rem(me + n_p - k, n_p)

    barrier = pltpu.get_barrier_semaphore()

    @pl.loop(1, n_p)
    def _(k):
        pl.semaphore_signal(barrier, inc=1, device_id=plane_id(peer(k)), device_id_type=MESH)

    @pl.loop(1, n_z)
    def _(k):
        pl.semaphore_signal(
            barrier, inc=1, device_id=(y, lax.rem(z + k, n_z), s), device_id_type=MESH
        )

    route = route_ref[...]
    onehot = (route == lax.broadcasted_iota(jnp.int32, (n_p, tok_count), 0)).astype(F32)
    token_row = lax.broadcasted_iota(jnp.int32, (tok_count, tok_count), 0)
    token_col = lax.broadcasted_iota(jnp.int32, (tok_count, tok_count), 1)
    earlier = (token_row < token_col).astype(F32).astype(BF16)
    ahead = jnp.dot(onehot.astype(BF16), earlier, preferred_element_type=F32)
    rank = jnp.sum(ahead * onehot, axis=0, keepdims=True).astype(jnp.int32)
    place = jnp.where(rank < cap, route * capp + rank, padded)
    dispatch = (place == lax.broadcasted_iota(jnp.int32, (padded, tok_count), 0)).astype(F32).astype(BF16)
    slots[0] = jnp.dot(dispatch, tok_ref[...], preferred_element_type=F32).astype(BF16)

    pl.semaphore_wait(barrier, n_p - 1 + n_z - 1)

    def padded_rows(q):
        return pl.ds(pl.multiple_of(q * capp, 16), capp)

    def block(o):
        return pl.ds(pl.multiple_of(o * blk, 16), blk)

    def chunk(o, c):
        return pl.ds(pl.multiple_of(o * blk + c * chk, 16), chk)

    part_p = n_p // n_c
    first = me // part_p

    def nth(t):
        return lax.rem(first + t, n_c)

    def plane_copy(i, k):
        return pltpu.make_async_remote_copy(
            src_ref=slots.at[i, padded_rows(peer(k))],
            dst_ref=arrived.at[i, padded_rows(me)],
            send_sem=a_send.at[i, k],
            recv_sem=a_recv.at[i, k],
            device_id=plane_id(peer(k)),
            device_id_type=MESH,
        )

    def plane_arrival(i, k):
        return pltpu.make_async_remote_copy(
            src_ref=slots.at[i, padded_rows(me)],
            dst_ref=arrived.at[i, padded_rows(source(k))],
            send_sem=a_send.at[i, k],
            recv_sem=a_recv.at[i, k],
            device_id=plane_id(peer(k)),
            device_id_type=MESH,
        )

    def start_plane(i):
        @pl.loop(0, n_p)
        def _(t):
            q = nth(t // part_p) * part_p + lax.rem(me + t, part_p)

            @pl.when(q != me)
            def _():
                plane_copy(i, lax.rem(q + n_p - me, n_p)).start()

        arrived[i, padded_rows(me), :] = slots[i, padded_rows(me), :]

    start_plane(0)

    logits = lax.dot_general(
        wr_ref[...], tok_ref[...], (((1,), (1,)), ((), ())), preferred_element_type=F32
    )
    gate_row = jax.nn.sigmoid(jnp.sum(logits * onehot, axis=0, keepdims=True))
    gate = jnp.sum(jnp.where(token_row == token_col, gate_row, 0.0), axis=1, keepdims=True)
    gated = (gate * cot_ref[...].astype(F32)).astype(BF16)
    slots[1] = jnp.dot(dispatch, gated, preferred_element_type=F32).astype(BF16)
    start_plane(1)

    part_pad = padded // n_c
    dense = lax.broadcasted_iota(jnp.int32, (chk, part_pad), 0)
    compact = (
        lax.broadcasted_iota(jnp.int32, (chk, part_pad), 1)
        == lax.div(dense, cap) * capp + lax.rem(dense, cap)
    ).astype(F32).astype(BF16)
    dense_t = lax.broadcasted_iota(jnp.int32, (part_pad, chk), 1)
    expand = (
        lax.broadcasted_iota(jnp.int32, (part_pad, chk), 0)
        == lax.div(dense_t, cap) * capp + lax.rem(dense_t, cap)
    ).astype(F32).astype(BF16)
    def part_rows(c):
        return pl.ds(pl.multiple_of(c * part_pad, 16), part_pad)

    def line_copy(i, o, c, to, sems):
        return pltpu.make_async_remote_copy(
            src_ref=rows.at[i, chunk(o, c)],
            dst_ref=rows.at[i, chunk(o, c)],
            send_sem=sems.at[i, o * n_c + c],
            recv_sem=z_recv.at[i, o * n_c + c],
            device_id=(y, to, s),
            device_id_type=MESH,
        )

    def send_right(i, o, c):
        @pl.when(z + 1 < n_z)
        def _():
            line_copy(i, o, c, z + 1, z_right).start()

    def send_left(i, o, c):
        @pl.when(z > 0)
        def _():
            line_copy(i, o, c, z - 1, z_left).start()

    def own_chunk(i, c):
        @pl.loop(0, part_p)
        def _(r):
            q = c * part_p + r

            @pl.when(q != me)
            def _():
                plane_arrival(i, lax.rem(me + n_p - q, n_p)).wait_recv()

        rows[i, chunk(z, c), :] = jnp.dot(
            compact, arrived[i, part_rows(c), :], preferred_element_type=F32
        ).astype(BF16)

    left_count, right_count = z, n_z - 1 - z

    def relay(s_at, c):
        @pl.when(jnp.logical_and(s_at >= 1, s_at <= 2 * left_count))
        def _():
            i = (s_at > left_count).astype(jnp.int32)
            o = z - s_at + i * left_count
            line_copy(i, o, c, z, z_right).wait_recv()
            send_right(i, o, c)

        @pl.when(jnp.logical_and(s_at >= 1, s_at <= 2 * right_count))
        def _():
            i = (s_at > right_count).astype(jnp.int32)
            o = z + s_at - i * right_count
            line_copy(i, o, c, z, z_left).wait_recv()
            send_left(i, o, c)

    low_end, high_end = z == 0, z == n_z - 1
    at_end = jnp.logical_or(low_end, high_end)

    def chain_copy(src, o, c, to, slot):
        return pltpu.make_async_remote_copy(
            src_ref=src.at[chunk(o, c)],
            dst_ref=rx.at[chunk(slot, c)],
            send_sem=c_send.at[o * n_c + c],
            recv_sem=c_recv.at[slot * n_c + c],
            device_id=(y, to, s),
            device_id_type=MESH,
        )

    def chain_send(src, o, c):
        @pl.when(z > o)
        def _():
            chain_copy(src, o, c, z - 1, o).start()

        @pl.when(z < o)
        def _():
            chain_copy(src, o, c, z + 1, jnp.where(z + 1 == o, n_z, o)).start()

    def forward(o):
        at = block(o)
        pre = jnp.dot(rows[0, at, :], win[...], preferred_element_type=F32)
        cdf = 0.5 * (1.0 + lax.erf(pre * (1.0 / math.sqrt(2.0))))
        act[at, :] = (pre * cdf).astype(BF16)
        slope[at, :] = cdf + pre * jnp.exp(-0.5 * pre * pre) * (1.0 / math.sqrt(2.0 * math.pi))
        part[at, :] = jnp.dot(act[at, :], wout[...], preferred_element_type=F32).astype(BF16)

    def backward():
        grad = lax.dot_general(
            rows[1], wout[...], (((1,), (1,)), ((), ())), preferred_element_type=F32
        )
        hg[...] = (grad * slope[...]).astype(BF16)

    def router_terms(o):
        own_rows = rows[0, block(o), :]
        row_logits = lax.dot_general(
            own_rows, wr_ref[...], (((1,), (1,)), ((), ())), preferred_element_type=F32
        )
        mine = (lax.broadcasted_iota(jnp.int32, row_logits.shape, 1) == me).astype(F32)
        row_gate = jax.nn.sigmoid(jnp.sum(row_logits * mine, axis=1, keepdims=True))
        inner = jnp.sum(
            rows[1, block(o), :].astype(F32) * part[block(o), :].astype(F32), axis=1, keepdims=True
        )
        vec[0] = vec[0] + jnp.sum(
            own_rows.astype(F32) * (inner * (1.0 - row_gate)), axis=0, keepdims=True
        )

    def send_cots(to_right, to_left):
        @pl.when(to_right)
        def _():
            @pl.loop(0, n_c)
            def _(t):
                send_right(1, z, nth(t))

        @pl.when(to_left)
        def _():
            @pl.loop(0, n_c)
            def _(t):
                send_left(1, z, nth(t))

    vec[...] = jnp.zeros_like(vec)

    @pl.loop(0, n_c)
    def _(t):
        own_chunk(0, nth(t))
        send_right(0, z, nth(t))
        send_left(0, z, nth(t))

    load_in.wait()
    load_out.wait()

    @pl.loop(0, 2 * n_z - 1)
    def _(k):
        @pl.loop(0, n_c)
        def _(t):
            relay(k, nth(t))

        send_cots(
            jnp.logical_and(k >= 1, k == left_count), jnp.logical_and(k >= 1, k == right_count)
        )

        @pl.loop(0, 2)
        def _(side):
            o = jnp.where(side == 0, z - k, z + k)

            @pl.when(jnp.logical_and(jnp.logical_and(o >= 0, o < n_z), k + 1 - side > 0))
            def _():
                forward(o)

            @pl.when(jnp.logical_and(at_end, jnp.logical_and(o >= 0, o < n_z)))
            def _():
                @pl.loop(0, n_c)
                def _(t):
                    @pl.when(k >= 2)
                    def _():
                        chain_send(part, o, nth(t))

                @pl.when(k == n_z - 1)
                def _():
                    @pl.loop(0, n_c)
                    def _(t):
                        chain_send(part, jnp.where(low_end, 1, n_z - 2), nth(t))

        @pl.when(k == 0)
        def _():
            @pl.loop(0, n_c)
            def _(t):
                own_chunk(1, nth(t))

        send_cots(
            jnp.logical_and(k == 0, left_count == 0), jnp.logical_and(k == 0, right_count == 0)
        )

        @pl.loop(0, 2)
        def _(side):
            count = jnp.where(side == 0, left_count, right_count)
            o = jnp.where(side == 0, z - k + count, z + k - count)
            arrived_now = jnp.logical_and(k > count, k <= 2 * count)

            @pl.when(jnp.logical_or(arrived_now, jnp.logical_and(k == 0, side == 0)))
            def _():
                router_terms(jnp.where(k == 0, z, o))

    outs = [
        pltpu.make_async_copy(rows.at[0], rows_out, o_sem.at[0]),
        pltpu.make_async_copy(act, act_out, o_sem.at[1]),
        pltpu.make_async_copy(rows.at[1], cots_out, o_sem.at[2]),
        pltpu.make_async_copy(hg, hg_out, o_sem.at[3]),
    ]
    outs[0].start()
    outs[1].start()
    outs[2].start()

    def vec_copy(k, slot):
        return pltpu.make_async_remote_copy(
            src_ref=vec.at[0], dst_ref=vec_z.at[slot], send_sem=v_send.at[k], recv_sem=v_recv.at[k],
            device_id=(y, lax.rem(z + k, n_z), s), device_id_type=MESH,
        )

    @pl.loop(1, n_z)
    def _(k):
        vec_copy(k, z).start()

    vec_z[z] = vec[0]

    def chain_step(o):
        @pl.loop(0, n_c)
        def _(t):
            c = nth(t)
            chain_copy(part, o, c, z, o).wait_recv()
            rx[chunk(o, c), :] = (
                part[chunk(o, c), :].astype(F32) + rx[chunk(o, c), :].astype(F32)
            ).astype(BF16)
            chain_send(rx, o, c)

    def chain_low():
        @pl.loop(1, n_z)
        def _(k):
            @pl.when(jnp.logical_and(z - k >= 0, z < n_z - 1))
            def _():
                chain_step(z - k)

    def chain_high():
        @pl.loop(1, n_z)
        def _(k):
            @pl.when(jnp.logical_and(z + k < n_z, z > 0))
            def _():
                chain_step(z + k)

    upper = 2 * z >= n_z

    @pl.when(upper)
    def _():
        chain_low()

    @pl.when(jnp.logical_not(upper))
    def _():
        chain_high()

    backward()
    outs[3].start()

    @pl.when(upper)
    def _():
        chain_high()

    @pl.when(jnp.logical_not(upper))
    def _():
        chain_low()

    def back_copy(k, q, there):
        return pltpu.make_async_remote_copy(
            src_ref=back_send.at[padded_rows(q)], dst_ref=back.at[padded_rows(there)],
            send_sem=b_send.at[k], recv_sem=b_recv.at[k],
            device_id=plane_id(q), device_id_type=MESH,
        )

    @pl.loop(0, n_c)
    def _(t):
        c = nth(t)

        @pl.when(z < n_z - 1)
        def _():
            chain_copy(part, z, c, z, z).wait_recv()

        @pl.when(z > 0)
        def _():
            chain_copy(part, z, c, z, n_z).wait_recv()

        from_right = jnp.where(z < n_z - 1, rx[chunk(z, c), :].astype(F32), 0.0)
        from_left = jnp.where(z > 0, rx[chunk(n_z, c), :].astype(F32), 0.0)
        final = (part[chunk(z, c), :].astype(F32) + from_right + from_left).astype(BF16)
        back_send[part_rows(c), :] = jnp.dot(expand, final, preferred_element_type=F32).astype(BF16)

        @pl.loop(0, part_p)
        def _(r):
            q = c * part_p + r

            @pl.when(q != me)
            def _():
                back_copy(lax.rem(q + n_p - me, n_p), q, me).start()

    back[padded_rows(me), :] = back_send[padded_rows(me), :]

    @pl.loop(1, n_z)
    def _(k):
        vec_copy(k, lax.rem(z + n_z - k, n_z)).wait_recv()

    vec_p[me] = jnp.sum(vec_z[...], axis=0) * scale

    def vec_plane(k, slot):
        return pltpu.make_async_remote_copy(
            src_ref=vec_p.at[me], dst_ref=vec_p.at[slot], send_sem=p_send.at[k], recv_sem=p_recv.at[k],
            device_id=plane_id(peer(k)), device_id_type=MESH,
        )

    @pl.loop(1, n_p)
    def _(k):
        vec_plane(k, me).start()

    @pl.loop(1, n_p)
    def _(k):
        back_copy(k, peer(k), source(k)).wait_recv()

    picked = lax.dot_general(
        dispatch, back[...], (((0,), (0,)), ((), ())), preferred_element_type=F32
    )
    moe_ref[...] = (gate * picked).astype(BF16)

    @pl.loop(1, n_p)
    def _(k):
        vec_plane(k, source(k)).wait_recv()

    for q in range(n_p):
        router_ref[q : q + 1, :] = vec_p[q]

    @pl.loop(1, n_p)
    def _(k):
        plane_copy(0, k).wait_send()
        plane_copy(1, k).wait_send()
        back_copy(k, peer(k), me).wait_send()
        vec_plane(k, me).wait_send()

    @pl.loop(1, n_z)
    def _(k):
        vec_copy(k, z).wait_send()

    @pl.loop(0, n_z)
    def _(o):
        @pl.loop(0, n_c)
        def _(c):
            @pl.when(jnp.logical_and(o <= z, z + 1 < n_z))
            def _():
                line_copy(0, o, c, z, z_right).wait_send()
                line_copy(1, o, c, z, z_right).wait_send()

            @pl.when(jnp.logical_and(o >= z, z > 0))
            def _():
                line_copy(0, o, c, z, z_left).wait_send()
                line_copy(1, o, c, z, z_left).wait_send()

            @pl.when(o != z)
            def _():
                chain_copy(part, o, c, z, o).wait_send()

    for out in outs:
        out.wait()


def gradient_kernel(
    scale,
    rows_hbm, hg_hbm, act_hbm, cots_hbm, moe_hbm, router_hbm,
    grad_in, grad_out, moe_out, router_out,
    rows, cots, act, hg, gin, gout, moe, router, in_sem, out_sem,
):
    loads = [
        pltpu.make_async_copy(act_hbm, act, in_sem.at[0]),
        pltpu.make_async_copy(cots_hbm, cots, in_sem.at[1]),
        pltpu.make_async_copy(rows_hbm, rows, in_sem.at[2]),
        pltpu.make_async_copy(hg_hbm, hg, in_sem.at[3]),
        pltpu.make_async_copy(moe_hbm, moe, in_sem.at[4]),
        pltpu.make_async_copy(router_hbm, router, in_sem.at[5]),
    ]
    for load in loads:
        load.start()
    stores = []

    def product(left, right, held, out, sem):
        count = left.shape[1]
        half = count // 2 if count % 256 == 0 else count
        for at in range(0, count, half):
            held[at : at + half, :] = (
                lax.dot_general(
                    left[:, at : at + half], right[...], (((0,), (0,)), ((), ())),
                    preferred_element_type=F32,
                )
                * scale
            ).astype(BF16)
            stores.append(
                pltpu.make_async_copy(
                    held.at[at : at + half], out.at[at : at + half], out_sem.at[sem + at // half]
                )
            )
            stores[-1].start()

    loads[0].wait()
    loads[1].wait()
    product(act, cots, gout, grad_out, 0)
    loads[4].wait()
    stores.append(pltpu.make_async_copy(moe, moe_out, out_sem.at[4]))
    stores[-1].start()
    loads[5].wait()
    stores.append(pltpu.make_async_copy(router, router_out, out_sem.at[5]))
    stores[-1].start()
    loads[2].wait()
    loads[3].wait()
    product(rows, hg, gin, grad_in, 2)
    for store in stores:
        store.wait()


def shards(tokens, routes, w_router, w_in, w_out, cotangent):
    tok_count, width = tokens.shape
    n_experts = w_router.shape[1]
    n_y, n_z, n_s = lax.axis_size("expert"), lax.axis_size("dp"), lax.axis_size("section")
    n_p = n_y * n_s
    cap = max(2, 3 * tok_count // (4 * n_experts))
    scale = math.sqrt(n_experts / (tok_count * n_y * n_z * n_s))
    capp = round_up(cap, 16)
    blk = round_up(n_p * cap, 16)
    n_c = 2 if n_p % 2 == 0 and n_p * cap % 32 == 0 else 1
    padded = n_p * capp
    hidden = w_in.shape[2]
    total = n_z * blk
    vmem = pl.BlockSpec(memory_space=pltpu.VMEM)
    hbm = pl.BlockSpec(memory_space=pl.ANY)
    dma = pltpu.SemaphoreType.DMA
    moe, router, rows, cots, act, hg = pl.pallas_call(
        functools.partial(exchange_kernel, (n_y, n_z, n_s, cap, capp, blk, n_c, scale)),
        out_shape=(
            jax.ShapeDtypeStruct((tok_count, width), BF16),
            jax.ShapeDtypeStruct((n_p, width), F32),
            jax.ShapeDtypeStruct((total, width), BF16),
            jax.ShapeDtypeStruct((total, width), BF16),
            jax.ShapeDtypeStruct((total, hidden), BF16),
            jax.ShapeDtypeStruct((total, hidden), BF16),
        ),
        in_specs=[vmem, vmem, vmem, vmem, hbm, hbm],
        out_specs=(vmem, vmem, hbm, hbm, hbm, hbm),
        scratch_shapes=[
            pltpu.VMEM((width, hidden), BF16),
            pltpu.VMEM((hidden, width), BF16),
            pltpu.VMEM((2, padded, width), BF16),
            pltpu.VMEM((2, padded, width), BF16),
            pltpu.VMEM((2, total, width), BF16),
            pltpu.VMEM((total, hidden), BF16),
            pltpu.VMEM((total, hidden), F32),
            pltpu.VMEM((total, hidden), BF16),
            pltpu.VMEM((total, width), BF16),
            pltpu.VMEM((total + blk, width), BF16),
            pltpu.VMEM((padded, width), BF16),
            pltpu.VMEM((padded, width), BF16),
            pltpu.VMEM((1, 1, width), F32),
            pltpu.VMEM((n_z, 1, width), F32),
            pltpu.VMEM((n_p, 1, width), F32),
            dma((2, n_p)), dma((2, n_p)),
            dma((2, n_z * n_c)), dma((2, n_z * n_c)), dma((2, n_z * n_c)),
            dma((n_z * n_c,)), dma(((n_z + 1) * n_c,)),
            dma((n_p,)), dma((n_p,)),
            dma((n_z,)), dma((n_z,)), dma((n_p,)), dma((n_p,)),
            dma((2,)), dma((4,)),
        ],
        compiler_params=pltpu.CompilerParams(
            collective_id=0, has_side_effects=True, vmem_limit_bytes=60 << 20
        ),
    )(tokens, routes.reshape(1, tok_count), w_router.T, cotangent, w_in[0], w_out[0])
    grad_in, grad_out, moe, router = pl.pallas_call(
        functools.partial(gradient_kernel, scale),
        out_shape=(
            jax.ShapeDtypeStruct((width, hidden), BF16),
            jax.ShapeDtypeStruct((hidden, width), BF16),
            jax.ShapeDtypeStruct((tok_count, width), BF16),
            jax.ShapeDtypeStruct((n_p, width), F32),
        ),
        in_specs=[hbm] * 6,
        out_specs=(hbm, hbm, hbm, hbm),
        scratch_shapes=[
            pltpu.VMEM((total, width), BF16),
            pltpu.VMEM((total, width), BF16),
            pltpu.VMEM((total, hidden), BF16),
            pltpu.VMEM((total, hidden), BF16),
            pltpu.VMEM((width, hidden), BF16),
            pltpu.VMEM((hidden, width), BF16),
            pltpu.VMEM((tok_count, width), BF16),
            pltpu.VMEM((n_p, width), F32),
            dma((6,)), dma((6,)),
        ],
        compiler_params=pltpu.CompilerParams(vmem_limit_bytes=60 << 20),
    )(rows, hg, act, cots, moe, router)
    return (moe, router.T, grad_in[None], grad_out[None])


def solution(mesh):
    return jax.shard_map(
        shards,
        mesh=mesh,
        in_specs=(
            P(("expert", "dp", "section"), None),
            P(("expert", "dp", "section"), None),
            P(),
            P(("expert", "section"), None, "dp"),
            P(("expert", "section"), "dp", None),
            P(("expert", "dp", "section"), None),
        ),
        out_specs=(
            P(("expert", "dp", "section"), None),
            P(),
            P(("expert", "section"), None, "dp"),
            P(("expert", "section"), "dp", None),
        ),
        check_vma=False,
    )
```
